256 devices in a mesh: row: 16 (over z_hi, y, core), col: 16 (over z_lo, x).
Axes of the slice: x: 4, y: 4, z: 8 (z_hi: 2, z_lo: 4; z = z_hi * 4 + z_lo), core: 2. Of those that a mesh axis runs over, the one named last changes fastest.
Arguments:
- raster: bfloat16 [64, 512, 2048], P(None, 'row', 'col')
- conv_one: bfloat16 [64, 576], replicated, may hold values from -0.25 to 0.25
- bias_one: float32 [64], replicated, may hold values from -3 to 3
- conv_two: bfloat16 [64, 576], replicated, may hold values from -0.25 to 0.25
- bias_two: float32 [64], replicated, may hold values from -3 to 3
- pos_embed: bfloat16 [64, 16, 64], P(None, 'row', 'col'), may hold values from -6 to 6
- query_embed: bfloat16 [2048, 256], replicated
- w_query: bfloat16 [256, 256], replicated, may hold values from -0.375 to 0.375
- w_key: bfloat16 [64, 256], replicated, may hold values from -0.75 to 0.75
- w_value: bfloat16 [64, 256], replicated, may hold values from -0.75 to 0.75
- w_out: bfloat16 [256, 256], replicated, may hold values from -0.375 to 0.375
- visible: int32 [16, 256], replicated, may hold values from 0 to 1, as said below
Outputs:
- map_queries: bfloat16 [2048, 256], P(('row', 'col'))
The draws below stay inside these ranges and needn't reach their ends.
Inputs may be any that keep to these rules, and one draw needn't show every extreme that they name: `visible`: every query block sees at least one tile; each block sees a square of tiles around one tile and, independently, about one in eight of the other tiles.
All inputs are finite; a program needn't handle non-finite values.
Results may differ from the reference program's by a relative error of at most 0.035.
Values may be sent and summed in bfloat16 or wider, within the bound.
No kernel may reach another device: no remote copies, remote signals or barrier semaphores. Data moves between devices by JAX's collectives and lax.ppermute only.
A program may use at most 128 MiB of HBM per device.

```python
import jax
import jax.numpy as jnp
from jax import lax

C = 64
E = 256
HEADS = 8
HEAD_DIM = 32
PATCH = 32
QBLOCK = 128
CELL_R = 32
CELL_C = 128
GRID_R = 512
GRID_C = 2048
PR = 16
PC = 64
QUERIES = 2048
NQB = 16
TILES = 256
N_ROW = 16
N_COL = 16


def draw_raster(key, part):
    key_base = jax.random.fold_in(key, 11)
    key_gain = jax.random.fold_in(key, 12)
    key_shift = jax.random.fold_in(key, 13)
    blocks_r = GRID_R // 16
    blocks_c = GRID_C // 16
    gain = jnp.exp(jax.random.uniform(key_gain, (C, blocks_r, 1, blocks_c, 1), jnp.float32, -1.5, 1.5))
    shift = jnp.clip(0.7 * jax.random.normal(key_shift, (C, blocks_r, 1, blocks_c, 1), jnp.float32), -2.5, 2.5)
    base = jnp.clip(jax.random.normal(key_base, (C, blocks_r, 16, blocks_c, 16), jnp.float32), -6.0, 6.0)
    return (base * gain + shift).reshape(C, GRID_R, GRID_C).astype(jnp.bfloat16)


def draw_query_embed(key, part):
    key_base = jax.random.fold_in(key, 21)
    return (2.5 * jnp.clip(jax.random.normal(key_base, (QUERIES, E), jnp.float32), -6.0, 6.0)).astype(jnp.bfloat16)


def draw_visible(key, part):
    center_r = jax.random.randint(jax.random.fold_in(key, 31), (NQB, 1), 0, N_ROW)
    center_c = jax.random.randint(jax.random.fold_in(key, 32), (NQB, 1), 0, N_COL)
    radius = jax.random.randint(jax.random.fold_in(key, 33), (NQB, 1), 1, 4)
    extra = jax.random.randint(jax.random.fold_in(key, 34), (NQB, TILES), 0, 8) == 0
    tile_r = jnp.arange(TILES, dtype=jnp.int32)[None, :] // N_COL
    tile_c = jnp.arange(TILES, dtype=jnp.int32)[None, :] % N_COL
    reach = jnp.maximum(jnp.abs(tile_r - center_r), jnp.abs(tile_c - center_c))
    return ((reach <= radius) | extra).astype(jnp.int32)


def steps_of(own_key, dims, pieces, low, high):
    level, own = 1.0, jax.random.fold_in(own_key, 6)
    for position, shards_of in pieces:
        draws = jnp.exp(jax.random.uniform(jax.random.fold_in(own, position), (shards_of,), jnp.float32, low / len(pieces), high / len(pieces)))
        level = level * jnp.repeat(draws, dims[position] // shards_of).reshape([-1 if axis == position else 1 for axis in range(len(dims))])
    return level


def noise(key, dims, scale, bound, split=(), held_as=jnp.bfloat16):
    factor_of = steps_of(key, dims, split, -0.22, 0.18) if split else 1.0
    drawn = jax.random.normal(key, dims, jnp.float32) * scale * factor_of
    return jnp.minimum(jnp.maximum(drawn, -bound), bound).astype(held_as)


def setup_inputs(seed: int = 0) -> dict:
    seeds = jax.random.split(jax.random.key(seed), 13)
    return {
        "raster": draw_raster(jax.random.fold_in(seeds[12], 71), 0),
        "conv_one": noise(seeds[1], (C, 9 * C), (9 * C) ** -0.5, 0.25),
        "bias_one": noise(seeds[2], (C,), 0.5, 3.0, (), jnp.float32),
        "conv_two": noise(seeds[3], (C, 9 * C), (9 * C) ** -0.5, 0.25),
        "bias_two": noise(seeds[4], (C,), 0.5, 3.0, (), jnp.float32),
        "pos_embed": noise(seeds[5], (C, PR, PC), 1.0, 6.0, ((1, 16), (2, 16))),
        "query_embed": draw_query_embed(jax.random.fold_in(seeds[12], 71), 0),
        "w_query": noise(seeds[7], (E, E), E ** -0.5, 0.375),
        "w_key": noise(seeds[8], (C, E), C ** -0.5, 0.75),
        "w_value": noise(seeds[9], (C, E), C ** -0.5, 0.75),
        "w_out": noise(seeds[10], (E, E), E ** -0.5, 0.375),
        "visible": draw_visible(jax.random.fold_in(seeds[12], 71), 0),
    }


def conv_valid(padded, weight, bias):
    height = padded.shape[1] - 2
    width = padded.shape[2] - 2
    taps = [padded[:, dy:dy + height, dx:dx + width] for dy in range(3) for dx in range(3)]
    stacked = jnp.concatenate(taps, 0).astype(jnp.float32)
    out = jnp.einsum("ok,khw->ohw", weight.astype(jnp.float32), stacked) + bias[:, None, None]
    return jnp.maximum(out, 0.0)


def reference(raster, conv_one, bias_one, conv_two, bias_two, pos_embed, query_embed, w_query, w_key, w_value, w_out, visible):
    padded = jnp.pad(raster, ((0, 0), (2, 2), (2, 2)))

    def strip(index):
        start = (index * PATCH).astype(jnp.int32)
        piece = lax.dynamic_slice(padded, (jnp.int32(0), start, jnp.int32(0)), (C, PATCH + 4, GRID_C + 4))
        first = conv_valid(piece, conv_one, bias_one)
        rows_glob = start - 1 + jnp.arange(PATCH + 2, dtype=jnp.int32)
        cols_glob = jnp.arange(GRID_C + 2, dtype=jnp.int32) - 1
        inside = ((rows_glob >= 0) & (rows_glob < GRID_R))[:, None] & ((cols_glob >= 0) & (cols_glob < GRID_C))[None, :]
        first = jnp.where(inside[None], first, 0.0).astype(jnp.bfloat16)
        second = conv_valid(first, conv_two, bias_two)
        return second.reshape(C, PATCH, PC, PATCH).mean(axis=(1, 3))

    pooled = lax.map(strip, jnp.arange(PR, dtype=jnp.int32))
    pooled = jnp.transpose(pooled, (1, 0, 2))
    tokens = (pooled + pos_embed.astype(jnp.float32)).astype(jnp.bfloat16)
    flat = tokens.reshape(C, PR * PC).T
    keys = jnp.dot(flat, w_key, preferred_element_type=jnp.float32).astype(jnp.bfloat16)
    values = jnp.dot(flat, w_value, preferred_element_type=jnp.float32).astype(jnp.bfloat16)
    queries = jnp.dot(query_embed, w_query, preferred_element_type=jnp.float32).astype(jnp.bfloat16)
    patch_row = jnp.arange(PR * PC, dtype=jnp.int32) // PC
    patch_col = jnp.arange(PR * PC, dtype=jnp.int32) % PC
    tile_of = (patch_row // (CELL_R // PATCH)) * N_COL + patch_col // (CELL_C // PATCH)
    key_heads = keys.reshape(PR * PC, HEADS, HEAD_DIM).astype(jnp.float32)
    value_heads = values.reshape(PR * PC, HEADS, HEAD_DIM).astype(jnp.float32)
    scale = 1.0 / (HEAD_DIM ** 0.5)

    def block(index):
        query_rows = lax.dynamic_slice_in_dim(queries, (index * QBLOCK).astype(jnp.int32), QBLOCK, 0)
        query_heads = query_rows.reshape(QBLOCK, HEADS, HEAD_DIM).astype(jnp.float32)
        seen = visible[index][tile_of] > 0
        score = jnp.einsum("qhd,khd->hqk", query_heads, key_heads) * scale
        peak = jnp.max(jnp.where(seen[None, None, :], score, -1e30), axis=-1)
        weight = jnp.where(seen[None, None, :], jnp.exp(score - peak[..., None]), 0.0)
        total = jnp.sum(weight, axis=-1)
        mixed = jnp.einsum("hqk,khd->qhd", weight.astype(jnp.bfloat16).astype(jnp.float32), value_heads)
        attended = (mixed / total.T[:, :, None]).reshape(QBLOCK, E).astype(jnp.bfloat16)
        return jnp.dot(attended, w_out, preferred_element_type=jnp.float32).astype(jnp.bfloat16)

    result = lax.map(block, jnp.arange(NQB, dtype=jnp.int32))
    return result.reshape(QUERIES, E)
```

```python
import functools

import jax
import jax.numpy as jnp
from jax import lax
from jax.experimental import pallas as pl
from jax.experimental.pallas import tpu as pltpu
from jax.sharding import PartitionSpec as P

E = 256
HEADS = 8
HEAD_DIM = 32
PATCH = 32
RIM = 2
F32 = jnp.float32
BF16 = jnp.bfloat16


def axis_pos():
    return lax.axis_index("row"), lax.axis_index("col")


def dot(a, b, dims=(((1,), (0,)), ((), ()))):
    return lax.dot_general(a, b, dims, preferred_element_type=F32)


def lanes(shape):
    return lax.broadcasted_iota(jnp.int32, shape, len(shape) - 1)


def sublanes(shape):
    return lax.broadcasted_iota(jnp.int32, shape, len(shape) - 2)


def call(kernel, out_shape, *args, flops=1 << 20, in_specs=None, scratch=()):
    if in_specs is None:
        in_specs = [pl.BlockSpec(memory_space=pltpu.VMEM)] * len(args)
    single = not isinstance(out_shape, (list, tuple))
    outs = [out_shape] if single else list(out_shape)
    result = pl.pallas_call(
        kernel,
        out_shape=outs,
        in_specs=in_specs,
        out_specs=[pl.BlockSpec(memory_space=pltpu.VMEM)] * len(outs),
        scratch_shapes=scratch,
        compiler_params=pltpu.CompilerParams(vmem_limit_bytes=24 << 20),
        cost_estimate=pl.CostEstimate(flops=flops, bytes_accessed=1 << 19, transcendentals=0),
    )(*args)
    return result[0] if single else result


def row_rim_kernel(upper_ref, lower_ref, first_ref, second_ref, up, low):
    r, _ = axis_pos()
    channels, height, width = upper_ref.shape
    up[...] = upper_ref[...].astype(F32).reshape(channels * height, width)
    low[...] = lower_ref[...].astype(F32).reshape(channels * height, width)
    even = lax.rem(r, 2) == 0
    for k in range(RIM):
        top = up[pl.ds(k, channels, stride=height), :]
        bottom = low[pl.ds(height - RIM + k, channels, stride=height), :]
        rows = pl.ds(k * channels, channels)
        first_ref[rows, :] = jnp.where(even, bottom, top).astype(BF16)
        second_ref[rows, :] = jnp.where(even, top, bottom).astype(BF16)


def strip_kernel(raster_ref, left_ref, right_ref, full):
    channels, rows, width = raster_ref.shape
    full[...] = raster_ref[...].astype(F32).reshape(channels * rows, width)
    where = lanes((channels, width))
    left = jnp.zeros((channels, width), F32)
    right = jnp.zeros((channels, width), F32)
    for h in range(rows):
        at = RIM * (h + RIM)
        piece = pltpu.roll(full[pl.ds(h, channels, stride=rows), :], at, 1)
        left = jnp.where((where >= at) & (where < at + RIM), piece, left)
        right = jnp.where((where >= at - RIM) & (where < at), piece, right)
    left_ref[...] = left
    right_ref[...] = pltpu.roll(right, RIM, 1)


def add_corners(strip, above, below, side, rows):
    channels, width = strip.shape
    where = lanes(strip.shape)
    for h, piece in [(k - RIM, above[k]) for k in range(RIM)] + [
        (rows + k, below[k]) for k in range(RIM)
    ]:
        at = RIM * (h + RIM)
        shift = at if side == 0 else (at + RIM) % width
        strip = jnp.where(
            (where >= at) & (where < at + RIM), pltpu.roll(piece, shift, 1), strip
        )
    return strip


def column_rim_kernel(
    rows, left_in, right_in, got_first, got_second, left_ref, right_ref, first_ref, second_ref, above_ref, below_ref
):
    r, c = axis_pos()
    channels = left_in.shape[0]
    even = lax.rem(r, 2) == 0
    above, below = [], []
    for k in range(RIM):
        part = pl.ds(k * channels, channels)
        one, two = got_first[part, :].astype(F32), got_second[part, :].astype(F32)
        above.append(jnp.where(even, two, one))
        below.append(jnp.where(even, one, two))
        above_ref[k] = above[k]
        below_ref[k] = below[k]
    left = add_corners(left_in[...], above, below, 0, rows)
    right = add_corners(right_in[...], above, below, 1, rows)
    left_ref[...] = left
    right_ref[...] = right
    even = lax.rem(c, 2) == 0
    first_ref[...] = jnp.where(even, right, left).astype(BF16)
    second_ref[...] = jnp.where(even, left, right).astype(BF16)


def conv_kernel(
    grid, raster_ref, above_ref, below_ref, own_left_ref, own_right_ref, got_first, got_second,
    one_ref, bias_one_ref, two_ref, bias_two_ref, pos_ref, out_ref, full, taps_one, taps_two,
):
    r, c = axis_pos()
    n_rows, n_cols = grid
    channels, rows, width = raster_ref.shape
    full[...] = raster_ref[...].astype(F32).reshape(channels * rows, width)
    shape = (channels, width)
    where = lanes(shape)
    even = lax.rem(c, 2) == 0
    one, two = got_first[...].astype(F32), got_second[...].astype(F32)
    far_left = jnp.where(even, two, one)
    far_right = jnp.where(even, one, two)

    def store_taps(taps, i, field, fill_left, fill_right):
        before = jnp.where(where == 0, fill_left, pltpu.roll(field, 1, 1))
        after = jnp.where(where == width - 1, fill_right, pltpu.roll(field, width - 1, 1))
        taps[i, 0:channels, :] = before.astype(BF16)
        taps[i, channels : 2 * channels, :] = field.astype(BF16)
        taps[i, 2 * channels : 3 * channels, :] = after.astype(BF16)

    def turn(x, shift):
        return pltpu.roll(x, shift % width, 1)

    for i in range(rows + 2 * RIM):
        h = i - RIM
        if h < 0:
            field = above_ref[i]
        elif h >= rows:
            field = below_ref[h - rows]
        else:
            field = full[pl.ds(h, channels, stride=rows), :]
        store_taps(
            taps_one, i, field,
            turn(far_left, -(RIM * i + RIM - 1)), turn(far_right, width - 1 - RIM * i),
        )

    weight_one, weight_two = one_ref[...], two_ref[...]
    bias_one = bias_one_ref[...]
    bias_two = bias_two_ref[...]

    own_left, own_right = own_left_ref[...], own_right_ref[...]
    left_taps = [far_left, turn(far_left, -1), own_left]
    right_taps = [turn(own_right, -1), far_right, turn(far_right, -1)]
    edge = jnp.concatenate(
        [
            jnp.concatenate([turn(a, -RIM * dy), turn(b, -RIM * dy)], axis=1).astype(BF16)
            for dy in (-1, 0, 1)
            for a, b in zip(left_taps, right_taps)
        ],
        axis=0,
    )
    edge_first = jnp.maximum(dot(weight_one, edge) + bias_one, 0.0)
    edge_left = jnp.where(c > 0, edge_first[:, :width], 0.0)
    edge_right = jnp.where(c < n_cols - 1, edge_first[:, width:], 0.0)

    def pair(taps, i):
        a = taps[i : i + 3].reshape(9 * channels, width)
        b = taps[i + 1 : i + 4].reshape(9 * channels, width)
        return jnp.concatenate([a, b], axis=1)

    for i in range(0, rows + 2, 2):
        both = jnp.maximum(dot(weight_one, pair(taps_one, i)) + bias_one, 0.0)
        for k in range(2):
            field = both[:, k * width : (k + 1) * width]
            at = RIM * (i + k + 1)
            fill_left, fill_right = turn(edge_left, -at), turn(edge_right, width - 1 - at)
            if i + k == 0 or i + k == rows + 1:
                keep = (r > 0) if i + k == 0 else (r < n_rows - 1)
                field = jnp.where(keep, field, 0.0)
                fill_left = jnp.where(keep, fill_left, 0.0)
                fill_right = jnp.where(keep, fill_right, 0.0)
            store_taps(taps_two, i + k, field, fill_left, fill_right)

    total = jnp.zeros((channels, 2 * width), F32)
    for i in range(0, rows, 2):
        total = total + jnp.maximum(dot(weight_two, pair(taps_two, i)) + bias_two, 0.0)
    total = total[:, :width] + total[:, width:]
    patches = width // PATCH
    member = (sublanes((8, width)) == lanes((8, width)) // PATCH).astype(F32)
    pooled = lax.dot_general(
        member, total, (((1,), (1,)), ((), ())),
        precision=lax.Precision.HIGHEST, preferred_element_type=F32,
    )
    tokens = pooled[:patches] * (1.0 / (PATCH * PATCH)) + pos_ref[...]
    flat = jnp.concatenate([tokens[k : k + 1] for k in range(patches)], axis=1)
    block = jnp.concatenate([flat[:, :128], flat[:, 128:]], axis=0).astype(BF16)
    out_ref[...] = jnp.broadcast_to(block[None], out_ref.shape)


def query_kernel(n_blocks, patches, embed_ref, w_query_ref, w_key_ref, visible_ref, out_ref, seen_ref):
    r, c = axis_pos()
    del c
    owned = embed_ref.shape[0]
    channels = w_key_ref.shape[0]
    queries = dot(embed_ref[...], w_query_ref[...]).astype(BF16).astype(F32)
    wide = jnp.concatenate([queries] * (patches * HEADS), axis=0)
    head = lax.rem(sublanes(wide.shape) // owned, HEADS)
    wide = jnp.where(head == lanes(wide.shape) // HEAD_DIM, wide, 0.0).astype(BF16)
    keys = jnp.concatenate([w_key_ref[...]] * patches, axis=0)
    folded = dot(wide, keys, (((1,), (1,)), ((), ()))) * (1.0 / HEAD_DIM**0.5)
    same = sublanes(folded.shape) // (HEADS * owned) == lanes(folded.shape) // channels
    out_ref[...] = jnp.where(same, folded, 0.0).astype(BF16)
    seen_ref[...] = visible_ref[pl.ds(r, 1), :]


def attend_kernel(folded_ref, seen_ref, tokens_ref, w_value_ref, w_out_ref, out_ref):
    owned = out_ref.shape[0]
    channels = w_value_ref.shape[0]
    tokens = tokens_ref[...]
    patches = tokens.shape[1] // channels
    group = HEADS * owned
    score = dot(folded_ref[...], tokens, (((1,), (1,)), ((), ())))
    seen = seen_ref[...] > 0
    score = jnp.where(seen, score, -1e30)
    parts = [score[p * group : (p + 1) * group] for p in range(patches)]
    peak = jnp.max(functools.reduce(jnp.maximum, parts), axis=1, keepdims=True)
    weights = [jnp.where(seen, jnp.exp(p - peak), 0.0) for p in parts]
    total = jnp.sum(functools.reduce(jnp.add, weights), axis=1, keepdims=True)
    stacked = jnp.concatenate(weights, axis=0).astype(BF16)
    mixed = dot(stacked, tokens)
    same = sublanes(mixed.shape) // group == lanes(mixed.shape) // channels
    mixed = jnp.where(same, mixed, 0.0)
    inverse = 1.0 / total
    mixed = (mixed * jnp.concatenate([inverse] * patches, axis=0)).astype(BF16)
    values = jnp.concatenate([w_value_ref[...]] * patches, axis=0)
    heads = dot(mixed, values)
    head = lax.rem(sublanes(heads.shape) // owned, HEADS)
    heads = jnp.where(head == lanes(heads.shape) // HEAD_DIM, heads, 0.0)
    attended = functools.reduce(
        jnp.add, [heads[k * owned : (k + 1) * owned] for k in range(patches * HEADS)]
    )
    out_ref[...] = dot(attended.astype(BF16), w_out_ref[...]).astype(BF16)


def swaps(n, start):
    pairs = [(i, i + 1) for i in range(start, n - 1, 2)]
    return pairs + [(j, i) for i, j in pairs]


def on_device(
    raster, conv_one, bias_one, conv_two, bias_two, pos_embed,
    query_embed, w_query, w_key, w_value, w_out, visible,
):
    channels, rows, width = raster.shape
    n_rows, n_cols = lax.axis_size("row"), lax.axis_size("col")
    devices = n_rows * n_cols
    patches = width // PATCH
    owned = query_embed.shape[0] // devices
    owner = lax.axis_index("row") * n_cols + lax.axis_index("col")
    tile = jax.ShapeDtypeStruct((channels, width), F32)
    half = jax.ShapeDtypeStruct((channels, width), BF16)
    rim = jax.ShapeDtypeStruct((RIM * channels, width), BF16)

    whole = pl.BlockSpec(memory_space=pltpu.VMEM)
    last = rows // 8 - 1
    first_rows, second_rows = pl.pallas_call(
        row_rim_kernel,
        grid=(1,),
        out_shape=[rim, rim],
        in_specs=[
            pl.BlockSpec((channels, 8, width), lambda i: (0, 0, 0)),
            pl.BlockSpec((channels, 8, width), lambda i: (0, last, 0)),
        ],
        out_specs=[whole, whole],
        scratch_shapes=[pltpu.VMEM((channels * 8, width), F32)] * 2,
        compiler_params=pltpu.CompilerParams(vmem_limit_bytes=24 << 20),
        cost_estimate=pl.CostEstimate(flops=1 << 20, bytes_accessed=1 << 18, transcendentals=0),
    )(raster, raster)
    got_first = lax.ppermute(first_rows, "row", swaps(n_rows, 0))
    got_second = lax.ppermute(second_rows, "row", swaps(n_rows, 1))
    left, right = call(
        strip_kernel, [tile, tile], raster, scratch=[pltpu.VMEM((channels * rows, width), F32)]
    )
    pair = jax.ShapeDtypeStruct((RIM, channels, width), F32)
    left, right, first_cols, second_cols, above, below = call(
        functools.partial(column_rim_kernel, rows),
        [tile, tile, half, half, pair, pair],
        left, right, got_first, got_second,
    )
    got_first = lax.ppermute(first_cols, "col", swaps(n_cols, 0))
    got_second = lax.ppermute(second_cols, "col", swaps(n_cols, 1))

    own_embed = lax.dynamic_slice_in_dim(query_embed, owner * owned, owned, 0)
    size = patches * HEADS * owned
    folded, seen = call(
        functools.partial(query_kernel, n_rows, patches),
        [
            jax.ShapeDtypeStruct((size, patches * channels), BF16),
            jax.ShapeDtypeStruct((1, devices), jnp.int32),
        ],
        own_embed, w_query, w_key, visible,
    )

    position = pos_embed.astype(F32).reshape(channels, patches).T
    block = call(
        functools.partial(conv_kernel, (n_rows, n_cols)),
        jax.ShapeDtypeStruct((devices, patches * channels // 128, 128), BF16),
        raster, above, below, left, right, got_first, got_second,
        conv_one, bias_one.reshape(channels, 1), conv_two, bias_two.reshape(channels, 1), position,
        flops=1 << 30,
        scratch=[
            pltpu.VMEM((channels * rows, width), F32),
            pltpu.VMEM((rows + 2 * RIM, 3 * channels, width), BF16),
            pltpu.VMEM((rows + 2, 3 * channels, width), BF16),
        ],
    )
    everyone = lax.all_to_all(block, ("row", "col"), 0, 0, tiled=True)
    tokens = everyone.reshape(devices, patches * channels)
    return call(
        attend_kernel,
        jax.ShapeDtypeStruct((owned, E), BF16),
        folded, seen, tokens, w_value, w_out,
    )


def solution(mesh):
    in_specs = (
        P(None, "row", "col"),
        P(),
        P(),
        P(),
        P(),
        P(None, "row", "col"),
        P(),
        P(),
        P(),
        P(),
        P(),
        P(),
    )
    out_specs = P(("row", "col"), None)
    return jax.shard_map(
        on_device, mesh=mesh, in_specs=in_specs, out_specs=out_specs, check_vma=False
    )
```
